32 devices in a mesh: dom: 2 (over x), frame: 16 (over z, y, core).
Axes of the slice: x: 2, y: 2, z: 4, core: 2. Of those that a mesh axis runs over, the one named last changes fastest.
Arguments:
- queries: bfloat16 [32, 512, 1024], P(('dom', 'frame')), parts along dimension 0, may hold values from -8 to 8
- keys: bfloat16 [32, 512, 1024], P(('dom', 'frame')), parts along dimension 0, may hold values from -8 to 8
- values: bfloat16 [32, 512, 1024], P(('dom', 'frame')), parts along dimension 0, may hold values from -6 to 6
- grad_out: bfloat16 [32, 512, 1024], P(('dom', 'frame')), parts along dimension 0, may hold values from -6 to 6
- links: int32 [32, 4], P(('dom', 'frame')), parts along dimension 0, may hold values from 0 to 1, as said below
- w_query: bfloat16 [1024, 1024], replicated, may hold values from -0.1875 to 0.1875
- w_key: bfloat16 [1024, 1024], replicated, may hold values from -0.1875 to 0.1875
- w_value: bfloat16 [1024, 1024], replicated, may hold values from -0.1875 to 0.1875
Outputs:
- grad_input: bfloat16 [32, 512, 1024], P(('dom', 'frame')), parts along dimension 0
The draws below stay inside these ranges and needn't reach their ends.
There are 2 independent parts, one for each index of `dom`. The reference program is written for one: setup_inputs(seed, part) draws one part's arguments, and reference() takes and returns one part's arrays. A program takes and returns all parts, laid end to end along the dimension named above; an argument that names none is the same for every part. Nothing has to cross between parts.
Inputs may be any that keep to these rules, and one draw needn't show every extreme that they name: links[t, j] is 0 whenever t < 2**j; otherwise 0 or 1, so frames attend to ragged numbers of up to 4 earlier frames.
All inputs are finite; a program needn't handle non-finite values.
Results may differ from the reference program's by a relative error of at most 0.0049.
Values may be sent and summed in bfloat16 or wider, within the bound.
A program may use at most 128 MiB of HBM per device.

```python
import jax
import jax.numpy as jnp
from jax import lax

D = 1024
HEADS = 16
PATCH = 512
NDIL = 4
FRAMES = 16


def base_draw(key, salt_value):
    sub_key = jax.random.fold_in(key, salt_value)
    return jnp.clip(jax.random.normal(sub_key, (FRAMES, PATCH, D), jnp.float32), -6.0, 6.0)


def draw_queries(key, part):
    base_field = base_draw(key, 1)
    return base_field.astype(jnp.bfloat16)


def draw_keys(key, part):
    base_field = base_draw(key, 2)
    return base_field.astype(jnp.bfloat16)


def draw_links(key, part):
    link_bits = jax.random.randint(jax.random.fold_in(key, 3), (FRAMES, NDIL), 0, 4)
    frame_ids = lax.broadcasted_iota(jnp.int32, (FRAMES, NDIL), 0)
    columns = lax.broadcasted_iota(jnp.int32, (FRAMES, NDIL), 1)
    spacings = jnp.left_shift(jnp.ones((FRAMES, NDIL), jnp.int32), columns)
    return jnp.where((link_bits > 0) & (frame_ids >= spacings), 1, 0).astype(jnp.int32)


def shard_levels(stream_key, dims, cuts, least, largest):
    loudness = 1.0
    for position, blocks in cuts:
        steps = jax.random.uniform(jax.random.fold_in(jax.random.fold_in(stream_key, 6), position), (blocks,), jnp.float32, least / len(cuts), largest / len(cuts))
        loudness = loudness * jnp.repeat(jnp.exp(steps), dims[position] // blocks).reshape((-1,) + (1,) * (len(dims) - 1 - position))
    return loudness


def gaussian(own_key, extent, width, bound, shards=(), dtype=jnp.bfloat16):
    level = shard_levels(own_key, extent, shards, -0.22, 0.18) if shards else 1.0
    result = jax.random.normal(own_key, extent, jnp.float32) * width * level
    return jnp.minimum(jnp.maximum(result, -bound), bound).astype(dtype)


def setup_inputs(seed: int = 0, part: int = 0) -> dict:
    arg_keys = jax.random.split(jax.random.key(seed), 9)
    part_keys = jax.random.split(jax.random.fold_in(arg_keys[8], part), 9)
    return {
        "queries": draw_queries(jax.random.fold_in(jax.random.fold_in(arg_keys[8], part), 71), part),
        "keys": draw_keys(jax.random.fold_in(jax.random.fold_in(arg_keys[8], part), 71), part),
        "values": gaussian(part_keys[2], (FRAMES, PATCH, D), 1.0, 6.0, ((0, 16),)),
        "grad_out": gaussian(part_keys[3], (FRAMES, PATCH, D), 1.0, 6.0, ((0, 16),)),
        "links": draw_links(jax.random.fold_in(jax.random.fold_in(arg_keys[8], part), 71), part),
        "w_query": gaussian(arg_keys[5], (D, D), D ** -0.5, 0.1875),
        "w_key": gaussian(arg_keys[6], (D, D), D ** -0.5, 0.1875),
        "w_value": gaussian(arg_keys[7], (D, D), D ** -0.5, 0.1875),
    }


def attention_core(query_f, grad_f, key_list, value_list, live_list, score_scale):
    live_mask = jnp.stack([m[:, None, None] for m in live_list])
    scores = jnp.stack([jnp.sum(query_f * k, axis=-1) for k in key_list]) * score_scale
    scores = jnp.where(live_mask > 0, scores, -1e30)
    highest = jnp.max(scores, axis=0)
    weights_raw = jnp.exp(scores - highest) * live_mask
    probability = weights_raw / jnp.sum(weights_raw, axis=0)
    grad_prob = jnp.stack([jnp.sum(grad_f * v, axis=-1) for v in value_list])
    inner_sum = jnp.sum(probability * grad_prob, axis=0)
    grad_score = probability * (grad_prob - inner_sum) * score_scale
    grad_query = jnp.zeros_like(query_f)
    grad_keys = []
    grad_values = []
    for i in range(len(key_list)):
        grad_query = grad_query + grad_score[i][..., None] * key_list[i]
        grad_keys.append(grad_score[i][..., None] * query_f)
        grad_values.append(probability[i][..., None] * grad_f)
    return grad_query, grad_keys, grad_values


def dot_transposed(left, weight):
    return lax.dot_general(left, weight, (((1,), (1,)), ((), ())), preferred_element_type=jnp.float32)


def reference(queries, keys, values, grad_out, links, w_query, w_key, w_value):
    frames, patches, model_width = queries.shape
    head_size = model_width // HEADS
    score_scale = head_size ** -0.5
    block_rows = 64 if patches % 64 == 0 else patches
    block_count = patches // block_rows

    def split_blocks(a):
        return a.reshape(frames, block_count, block_rows, model_width).transpose(1, 0, 2, 3)

    def spread_heads(a):
        return a.astype(jnp.float32).reshape(frames, block_rows, HEADS, head_size)

    def per_block(pieces):
        query_b, key_b, value_b, grad_b = pieces
        query_f = spread_heads(query_b)
        grad_f = spread_heads(grad_b)
        key_f = spread_heads(key_b)
        value_f = spread_heads(value_b)
        key_list = [key_f]
        value_list = [value_f]
        live_list = [jnp.ones((frames,), jnp.float32)]
        for j in range(NDIL):
            spacing = 2 ** j
            padding = jnp.zeros((spacing, block_rows, HEADS, head_size), jnp.float32)
            key_list.append(jnp.concatenate([padding, key_f[:frames - spacing]], axis=0))
            value_list.append(jnp.concatenate([padding, value_f[:frames - spacing]], axis=0))
            live_list.append((links[:, j] > 0).astype(jnp.float32))
        grad_query, grad_keys, grad_values = attention_core(query_f, grad_f, key_list, value_list, live_list, score_scale)
        key_total = grad_keys[0]
        value_total = grad_values[0]
        for j in range(NDIL):
            spacing = 2 ** j
            padding = jnp.zeros((spacing, block_rows, HEADS, head_size), jnp.float32)
            key_total = key_total + jnp.concatenate([grad_keys[j + 1][spacing:], padding], axis=0)
            value_total = value_total + jnp.concatenate([grad_values[j + 1][spacing:], padding], axis=0)
        shape_out = (frames, block_rows, model_width)
        return (grad_query.reshape(shape_out).astype(jnp.bfloat16),
                key_total.reshape(shape_out).astype(jnp.bfloat16),
                value_total.reshape(shape_out).astype(jnp.bfloat16))

    grad_query, grad_key, grad_value = lax.map(
        per_block, (split_blocks(queries), split_blocks(keys), split_blocks(values), split_blocks(grad_out)))

    def join_blocks(a):
        return a.transpose(1, 0, 2, 3).reshape(frames * patches, model_width)

    total = dot_transposed(join_blocks(grad_query), w_query)
    total = total + dot_transposed(join_blocks(grad_key), w_key)
    total = total + dot_transposed(join_blocks(grad_value), w_value)
    return total.reshape(frames, patches, model_width).astype(jnp.bfloat16)
```

```python
import functools

import jax
import jax.numpy as jnp
from jax import lax
from jax.experimental import pallas as pl
from jax.experimental.pallas import tpu as pltpu
from jax.sharding import PartitionSpec as P

HEADS = 16
NDIL = 4
LANES = 128
AHEAD = 3


def dot_nt(left, right):
    return lax.dot_general(
        left, right, (((1,), (1,)), ((), ())), preferred_element_type=jnp.float32
    )


def dot_nn(left, right):
    return lax.dot_general(
        left, right, (((1,), (0,)), ((), ())), preferred_element_type=jnp.float32
    )


def kernel(n, chunks, rows, links_ref, q_ref, k_ref, v_ref, g_ref, wq_ref, wk_ref, wv_ref,
           out_ref, own, slots, msg_out, msg_in, prods, gather, spread, weights,
           own_sem, w_sem, send_sem, recv_sem, msg_send, msg_recv):
    width = q_ref.shape[-1]
    head = width // HEADS
    scale = head ** (-0.5)
    half = rows // 2
    i = lax.axis_index("frame")
    f32, bf16 = jnp.float32, jnp.bfloat16

    def place(stream):
        return (i, 1) if stream == 0 else (n - 1 - i, -1)

    def load(stream, part, c):
        src = ((k_ref, v_ref), (q_ref, g_ref))[stream][part]
        return pltpu.make_async_copy(
            src.at[0, pl.ds(pl.multiple_of(c * rows, rows), rows), :],
            own.at[stream, c, part], own_sem.at[stream, part, c])

    def hop(stream, kind, c):
        m, sign = place(stream)
        bit1, bit0 = (m // 2) % 2, m % 2
        mine = own.at[stream, c]
        src, slot, off, cond = (
            (mine, 2, 4, m + 4 < n),
            (mine, 1, 2, bit1 == 0),
            (mine, 0, 1, bit0 == 0),
            (slots.at[stream, 2, c], 3, 4, jnp.logical_and(m >= 4, m + 4 < n)),
            (slots.at[stream, 2, c], 1, -2, jnp.logical_and(m >= 4, bit1 == 1)),
            (slots.at[stream, 1, c], 0, -1, jnp.logical_and(m >= 2, bit0 == 1)),
        )[kind]
        copy = pltpu.make_async_remote_copy(
            src_ref=src, dst_ref=slots.at[stream, slot, c],
            send_sem=send_sem.at[stream, kind, c], recv_sem=recv_sem.at[stream, slot, c],
            device_id={"frame": i + sign * off}, device_id_type=pl.DeviceIdType.MESH)
        return copy, cond

    def send(stream, kind, c):
        copy, cond = hop(stream, kind, c)

        @pl.when(cond)
        def _():
            copy.start()

    def arrive(stream, slot, c):
        m, sign = place(stream)

        @pl.when(m >= 2**slot)
        def _():
            pltpu.make_async_remote_copy(
                src_ref=own.at[stream, c], dst_ref=slots.at[stream, slot, c],
                send_sem=send_sem.at[stream, 0, c], recv_sem=recv_sem.at[stream, slot, c],
                device_id={"frame": i - sign * 2**slot},
                device_id_type=pl.DeviceIdType.MESH).wait_recv()

    def message(j, c):
        return pltpu.make_async_remote_copy(
            src_ref=msg_out.at[c, j + 1], dst_ref=msg_in.at[c, j],
            send_sem=msg_send.at[j, c], recv_sem=msg_recv.at[j, c],
            device_id={"frame": i - 2**j}, device_id_type=pl.DeviceIdType.MESH)

    for c in range(chunks):
        for stream in range(2):
            for part in range(2):
                load(stream, part, c).start()
    w_copies = [pltpu.make_async_copy(w, weights.at[x], w_sem.at[x])
                for x, w in enumerate((wq_ref, wk_ref, wv_ref))]
    for copy in w_copies:
        copy.start()

    barrier = pltpu.get_barrier_semaphore()
    peers = jnp.int32(0)
    for j in range(NDIL):
        for off in (2**j, -(2**j)):
            there = jnp.logical_and(i + off >= 0, i + off < n)
            peers = peers + there.astype(jnp.int32)

            @pl.when(there)
            def _():
                pl.semaphore_signal(barrier, inc=1, device_id={"frame": i + off},
                                    device_id_type=pl.DeviceIdType.MESH)
    pl.semaphore_wait(barrier, peers)

    def direct(c):
        for stream in range(2):
            for part in range(2):
                load(stream, part, c).wait()
        for kind in range(3):
            for stream in range(2):
                send(stream, kind, c)

    for c in range(min(AHEAD, chunks)):
        direct(c)

    feature = lax.broadcasted_iota(jnp.int32, (width, LANES), 0) // head
    lane = lax.broadcasted_iota(jnp.int32, (width, LANES), 1) % HEADS
    gather[...] = jnp.where(feature == lane, 1.0, 0.0).astype(bf16)
    lane = lax.broadcasted_iota(jnp.int32, (LANES, width), 0)
    feature = lax.broadcasted_iota(jnp.int32, (LANES, width), 1) // head
    for x in range(4):
        hit = jnp.logical_and(lane % HEADS == feature, lane // (2 * HEADS) == x)
        spread[x] = jnp.where(hit, 1.0, 0.0).astype(bf16)

    for stream in range(2):
        m, _ = place(stream)
        for j in range(NDIL):
            @pl.when(m < 2**j)
            def _():
                for c in range(chunks):
                    for part in range(2):
                        slots[stream, j, c, part] = jnp.zeros((rows, width), bf16)
                    if stream == 1:
                        msg_in[c, j] = jnp.zeros((half, LANES), bf16)
    for copy in w_copies:
        copy.wait()

    def relay_far(c):
        for stream in range(2):
            arrive(stream, 2, c)
            send(stream, 4, c)
            send(stream, 3, c)

    def relay_near(c):
        for stream in range(2):
            arrive(stream, 1, c)
            send(stream, 5, c)

    def attend(c):
        for slot in (0, 3):
            arrive(0, slot, c)
        for part in range(2):
            left = own[1, c, part].astype(f32)
            for j in range(NDIL + 1):
                right = own[0, c, part] if j == 0 else slots[0, j - 1, c, part]
                product = left * right.astype(f32)
                high = product.astype(bf16)
                low = (product - high.astype(f32)).astype(bf16)
                at = (part * (NDIL + 1) + j) * 2 * rows
                prods[at:at + rows] = high
                prods[at + rows:at + 2 * rows] = low
        sums = dot_nn(prods[...], gather[...])

        def reduced(part, j):
            at = (part * (NDIL + 1) + j) * 2 * rows
            return sums[at:at + rows] + sums[at + rows:at + 2 * rows]

        live = [None] + [(links_ref[0, j] > 0).astype(f32) for j in range(NDIL)]
        scores = [reduced(0, j) * scale for j in range(NDIL + 1)]
        scores = [s if j == 0 else jnp.where(live[j] > 0, s, -1e30)
                  for j, s in enumerate(scores)]
        highest = functools.reduce(jnp.maximum, scores)
        raw = [jnp.exp(s - highest) for s in scores]
        raw = [r if j == 0 else r * live[j] for j, r in enumerate(raw)]
        total = functools.reduce(jnp.add, raw)
        probability = [r / total for r in raw]
        grad_prob = [reduced(1, j) for j in range(NDIL + 1)]
        inner = functools.reduce(
            jnp.add, [p * g for p, g in zip(probability, grad_prob)])
        lanes = lax.broadcasted_iota(jnp.int32, (rows, LANES), 1)
        group = (lanes // HEADS) % 4
        lower = lanes[:half] < LANES // 2
        for j in range(NDIL + 1):
            prob = probability[j]
            grad_score = prob * (grad_prob[j] - inner) * scale
            value = jnp.where(group < 2, grad_score, prob)
            high = value.astype(bf16).astype(f32)
            value = jnp.where(group % 2 == 0, high, value - high)
            msg_out[c, j] = jnp.where(lower, value[:half], value[half:]).astype(bf16)
        for j in range(NDIL):
            @pl.when(i >= 2**j)
            def _():
                message(j, c).start()

    def finish(c):
        packed = msg_out[c].reshape((NDIL + 1) * half, LANES)
        halves = []
        for h in range(2):
            at = slice(h * half, (h + 1) * half)
            score = dot_nn(packed, spread[2 * h])
            total = score[:half] * own[0, c, 0, at].astype(f32)
            for j in range(NDIL):
                total += (score[(j + 1) * half:(j + 2) * half]
                          * slots[0, j, c, 0, at].astype(f32))
            halves.append(total.astype(bf16))
        result = dot_nt(jnp.concatenate(halves, axis=0), weights[0])

        for slot in (0, 3):
            arrive(1, slot, c)
        for j in range(NDIL):
            @pl.when(i + 2**j < n)
            def _():
                message(j, c).wait_recv()
        packed = jnp.concatenate(
            [msg_out[c, 0], msg_in[c].reshape(NDIL * half, LANES)], axis=0)
        for part in range(2):
            halves = []
            for h in range(2):
                at = slice(h * half, (h + 1) * half)
                factor = dot_nn(packed, spread[2 * h + part])
                total = factor[:half] * own[1, c, part, at].astype(f32)
                for j in range(NDIL):
                    total += (factor[(j + 1) * half:(j + 2) * half]
                              * slots[1, j, c, part, at].astype(f32))
                halves.append(total.astype(bf16))
            result += dot_nt(jnp.concatenate(halves, axis=0), weights[1 + part])
        out_ref[0, pl.ds(pl.multiple_of(c * rows, rows), rows), :] = result.astype(bf16)

    def step(s, carry):
        @pl.when(s < chunks)
        def _():
            relay_far(s)

        @pl.when(s + AHEAD < chunks)
        def _():
            direct(s + AHEAD)

        @pl.when(jnp.logical_and(s >= 1, s < chunks + 1))
        def _():
            relay_near(s - 1)

        @pl.when(jnp.logical_and(s >= 2, s < chunks + 2))
        def _():
            attend(s - 2)

        @pl.when(s >= 3)
        def _():
            finish(s - 3)
        return carry

    lax.fori_loop(0, chunks + 3, step, 0)

    def drain(c, carry):
        for stream in range(2):
            for kind in range(6):
                copy, cond = hop(stream, kind, c)

                @pl.when(cond)
                def _():
                    copy.wait_send()
        for j in range(NDIL):
            @pl.when(i >= 2**j)
            def _():
                message(j, c).wait_send()
        return carry

    lax.fori_loop(0, chunks, drain, 0)


def per_device(queries, keys, values, grad_out, links, w_query, w_key, w_value):
    frames, patches, width = queries.shape
    n = lax.axis_size("frame")
    rows = 64
    chunks = patches // rows
    half = rows // 2
    hbm = pl.BlockSpec(memory_space=pl.ANY)
    bf16 = jnp.bfloat16
    dma = pltpu.SemaphoreType.DMA
    return pl.pallas_call(
        functools.partial(kernel, n, chunks, rows),
        out_shape=jax.ShapeDtypeStruct((frames, patches, width), bf16),
        in_specs=[pl.BlockSpec(memory_space=pltpu.SMEM)] + [hbm] * 7,
        out_specs=pl.BlockSpec(memory_space=pltpu.VMEM),
        scratch_shapes=[
            pltpu.VMEM((2, chunks, 2, rows, width), bf16),
            pltpu.VMEM((2, NDIL, chunks, 2, rows, width), bf16),
            pltpu.VMEM((chunks, NDIL + 1, half, LANES), bf16),
            pltpu.VMEM((chunks, NDIL, half, LANES), bf16),
            pltpu.VMEM(((NDIL + 1) * 4 * rows, width), bf16),
            pltpu.VMEM((width, LANES), bf16),
            pltpu.VMEM((4, LANES, width), bf16),
            pltpu.VMEM((3, width, width), bf16),
            dma((2, 2, chunks)),
            dma((3,)),
            dma((2, 6, chunks)),
            dma((2, NDIL, chunks)),
            dma((NDIL, chunks)),
            dma((NDIL, chunks)),
        ],
        compiler_params=pltpu.CompilerParams(
            collective_id=0, has_side_effects=True, vmem_limit_bytes=60 * 1024 * 1024),
    )(links, queries, keys, values, grad_out, w_query, w_key, w_value)


def solution(mesh):
    placed = (
        P(("dom", "frame"), None, None),
        P(("dom", "frame"), None, None),
        P(("dom", "frame"), None, None),
        P(("dom", "frame"), None, None),
        P(("dom", "frame"), None),
        P(),
        P(),
        P(),
    )
    return jax.shard_map(
        per_device,
        mesh=mesh,
        in_specs=placed,
        out_specs=P(("dom", "frame"), None, None),
        check_vma=False,
    )
```

```python
import functools

import jax
import jax.numpy as jnp
from jax import lax
from jax.experimental import pallas as pl
from jax.experimental.pallas import tpu as pltpu
from jax.sharding import PartitionSpec as P

HEADS = 16
NDIL = 4
LANES = 128
AHEAD = 3
LAGS = (0, 1, 2, 3, 4, 5)


def dot_nt(left, right):
    return lax.dot_general(
        left, right, (((1,), (1,)), ((), ())), preferred_element_type=jnp.float32
    )


def dot_nn(left, right):
    return lax.dot_general(
        left, right, (((1,), (0,)), ((), ())), preferred_element_type=jnp.float32
    )


def kernel(n, chunks, rows, links_ref, q_ref, k_ref, v_ref, g_ref, wq_ref, wk_ref, wv_ref,
           out_ref, ahead, back, local, ahead_in, back_in, part_out, part_in,
           prob_out, prob_in, dot_out, dot_in, kept, kept_mid, kept_near, base,
           prods, gather, spread, fold, weights,
           own_sem, w_sem, send_sem, recv_sem, prob_send, prob_recv, dot_send, dot_recv,
           part_send, part_recv):
    width = q_ref.shape[-1]
    head = width // HEADS
    scale = head ** (-0.5)
    half = rows // 2
    count = NDIL + 1
    i = lax.axis_index("frame")
    f32, bf16 = jnp.float32, jnp.bfloat16

    own = (ahead, back)
    slots = (ahead_in, back_in)

    def place(stream):
        return (i, 1) if stream == 0 else (n - 1 - i, -1)

    def loads(c):
        plan = ((k_ref, 0, ahead, 0), (k_ref, 1, ahead, 1), (v_ref, 1, ahead, 2),
                (q_ref, 0, back, 0), (g_ref, 0, back, 1),
                (v_ref, 0, local, 0), (q_ref, 1, local, 1), (g_ref, 1, local, 2))
        return [pltpu.make_async_copy(
            src.at[0, pl.ds(pl.multiple_of((2 * c + side) * rows, rows), rows), :],
            dst.at[c, part], own_sem.at[x, c])
            for x, (src, side, dst, part) in enumerate(plan)]

    def hop(stream, kind, c):
        m, sign = place(stream)
        bit1, bit0 = (m // 2) % 2, m % 2
        mine, into = own[stream].at[c], slots[stream]
        src, slot, off, cond = (
            (mine, 2, 4, m + 4 < n),
            (mine, 1, 2, bit1 == 0),
            (mine, 0, 1, bit0 == 0),
            (into.at[2, c], 3, 4, jnp.logical_and(m >= 4, m + 4 < n)),
            (into.at[2, c], 1, -2, jnp.logical_and(m >= 4, bit1 == 1)),
            (into.at[1, c], 0, -1, jnp.logical_and(m >= 2, bit0 == 1)),
        )[kind]
        copy = pltpu.make_async_remote_copy(
            src_ref=src, dst_ref=into.at[slot, c],
            send_sem=send_sem.at[stream, kind, c], recv_sem=recv_sem.at[stream, slot, c],
            device_id={"frame": i + sign * off}, device_id_type=pl.DeviceIdType.MESH)
        return copy, cond

    def send(stream, kind, c):
        copy, cond = hop(stream, kind, c)

        @pl.when(cond)
        def _():
            copy.start()

    def arrive(stream, slot, c):
        m, sign = place(stream)

        @pl.when(m >= 2**slot)
        def _():
            pltpu.make_async_remote_copy(
                src_ref=own[stream].at[c], dst_ref=slots[stream].at[slot, c],
                send_sem=send_sem.at[stream, 0, c], recv_sem=recv_sem.at[stream, slot, c],
                device_id={"frame": i - sign * 2**slot},
                device_id_type=pl.DeviceIdType.MESH).wait_recv()

    def returns(slot):
        bit1, bit0 = (i // 2) % 2, i % 2
        if slot == 2:
            return [(0, -4, i >= 4)]
        if slot == 3:
            return [(3, -4, i >= 8)]
        if slot == 1:
            return [(1, -2, jnp.logical_and(i >= 2, bit1 == 1)),
                    (4, 2, jnp.logical_and(i >= 2, bit1 == 0))]
        return [(2, -1, bit0 == 1), (5, 1, jnp.logical_and(i >= 1, bit0 == 0))]

    def back_copy(slot, kind, off, c):
        return pltpu.make_async_remote_copy(
            src_ref=part_out.at[slot, c], dst_ref=part_in.at[kind, c],
            send_sem=part_send.at[slot, c], recv_sem=part_recv.at[kind, c],
            device_id={"frame": i + off}, device_id_type=pl.DeviceIdType.MESH)

    def give_back(slot, c):
        for kind, off, cond in returns(slot):
            @pl.when(cond)
            def _():
                back_copy(slot, kind, off, c).start()

    def add_back(kind, c, ref):
        cond = hop(0, kind, c)[1]
        off = (4, 2, 1, 4, -2, -1)[kind]

        @pl.when(cond)
        def _():
            pltpu.make_async_remote_copy(
                src_ref=part_out.at[0, c], dst_ref=part_in.at[kind, c],
                send_sem=part_send.at[0, c], recv_sem=part_recv.at[kind, c],
                device_id={"frame": i + off},
                device_id_type=pl.DeviceIdType.MESH).wait_recv()
            ref[c] += part_in[kind, c].astype(f32)

    def prob_copy(j, c):
        return pltpu.make_async_remote_copy(
            src_ref=prob_out.at[c, j + 1], dst_ref=prob_in.at[c, j],
            send_sem=prob_send.at[j, c], recv_sem=prob_recv.at[j, c],
            device_id={"frame": i - 2**j}, device_id_type=pl.DeviceIdType.MESH)

    def dot_copy(j, c):
        return pltpu.make_async_remote_copy(
            src_ref=dot_out.at[c, j], dst_ref=dot_in.at[c, j],
            send_sem=dot_send.at[j, c], recv_sem=dot_recv.at[j, c],
            device_id={"frame": i + 2**j}, device_id_type=pl.DeviceIdType.MESH)

    for c in range(chunks):
        for copy in loads(c):
            copy.start()
    w_copies = [pltpu.make_async_copy(w, weights.at[x], w_sem.at[x])
                for x, w in enumerate((wq_ref, wk_ref, wv_ref))]
    for copy in w_copies:
        copy.start()

    barrier = pltpu.get_barrier_semaphore()
    peers = jnp.int32(0)
    for j in range(NDIL):
        for off in (2**j, -(2**j)):
            there = jnp.logical_and(i + off >= 0, i + off < n)
            peers = peers + there.astype(jnp.int32)

            @pl.when(there)
            def _():
                pl.semaphore_signal(barrier, inc=1, device_id={"frame": i + off},
                                    device_id_type=pl.DeviceIdType.MESH)
    pl.semaphore_wait(barrier, peers)

    def direct(c):
        for copy in loads(c):
            copy.wait()
        for kind in range(3):
            for stream in range(2):
                send(stream, kind, c)

    for c in range(min(AHEAD, chunks)):
        direct(c)

    feature = lax.broadcasted_iota(jnp.int32, (width, LANES), 0) // head
    lane = lax.broadcasted_iota(jnp.int32, (width, LANES), 1) % HEADS
    gather[...] = jnp.where(feature == lane, 1.0, 0.0).astype(bf16)
    lane = lax.broadcasted_iota(jnp.int32, (LANES, width), 0)
    feature = lax.broadcasted_iota(jnp.int32, (LANES, width), 1) // head
    for x in range(4):
        hit = jnp.logical_and(lane % HEADS == feature, lane // (2 * HEADS) == x)
        spread[x] = jnp.where(hit, 1.0, 0.0).astype(bf16)
    lane = lax.broadcasted_iota(jnp.int32, (LANES, LANES), 0)
    feature = lax.broadcasted_iota(jnp.int32, (LANES, LANES), 1)
    for x in range(2):
        hit = jnp.logical_and(lane % HEADS == feature % HEADS, lane // (2 * HEADS) == 2 * x)
        fold[x] = jnp.where(hit, 1.0, 0.0).astype(bf16)

    for j in range(NDIL):
        @pl.when(i < 2**j)
        def _():
            for c in range(chunks):
                for part in range(3):
                    ahead_in[j, c, part] = jnp.zeros((rows, width), bf16)
                dot_in[c, j] = jnp.zeros((half, LANES), bf16)

        @pl.when(i + 2**j >= n)
        def _():
            for c in range(chunks):
                for part in range(2):
                    back_in[j, c, part] = jnp.zeros((rows, width), bf16)
                prob_in[c, j] = jnp.zeros((half, LANES), bf16)
    for copy in w_copies:
        copy.wait()

    lanes = lax.broadcasted_iota(jnp.int32, (rows, LANES), 1)
    group = (lanes // HEADS) % 4
    lower = lanes[:half] < LANES // 2

    def pack(value):
        return jnp.where(lower, value[:half], value[half:]).astype(bf16)

    def softmax_back(scores, grad_prob):
        live = [None] + [(links_ref[0, j] > 0).astype(f32) for j in range(NDIL)]
        scores = [s if j == 0 else jnp.where(live[j] > 0, s, -1e30)
                  for j, s in enumerate(scores)]
        highest = functools.reduce(jnp.maximum, scores)
        raw = [jnp.exp(s - highest) for s in scores]
        raw = [r if j == 0 else r * live[j] for j, r in enumerate(raw)]
        total = functools.reduce(jnp.add, raw)
        probability = [r / total for r in raw]
        inner = functools.reduce(
            jnp.add, [p * g for p, g in zip(probability, grad_prob)])
        values = []
        for prob, grad in zip(probability, grad_prob):
            grad_score = prob * (grad - inner) * scale
            value = jnp.where(group < 2, grad_score, prob)
            high = value.astype(bf16).astype(f32)
            values.append(jnp.where(group % 2 == 0, high, value - high))
        return values

    def relay_far(c):
        for stream in range(2):
            arrive(stream, 2, c)
            send(stream, 4, c)
            send(stream, 3, c)

    def relay_near(c):
        for stream in range(2):
            arrive(stream, 1, c)
            send(stream, 5, c)

    def query_grad(values, part, c):
        stack = jnp.concatenate([v.astype(bf16) for v in values], axis=0)
        factor = dot_nn(stack, spread[0])
        total = factor[:rows] * ahead[c, part].astype(f32)
        for j in range(NDIL):
            total += (factor[(j + 1) * rows:(j + 2) * rows]
                      * ahead_in[j, c, part].astype(f32))
        return total.astype(bf16), stack, factor

    def attend(c):
        for slot in (0, 3):
            for stream in range(2):
                arrive(stream, slot, c)
        pairs = (
            [(back[c, 0], ahead[c, 0])]
            + [(back[c, 0], ahead_in[j, c, 0]) for j in range(NDIL)]
            + [(back[c, 1], local[c, 0])]
            + [(back_in[j, c, 1], local[c, 0]) for j in range(NDIL)]
            + [(local[c, 1], ahead[c, 1])]
            + [(local[c, 1], ahead_in[j, c, 1]) for j in range(NDIL)]
            + [(local[c, 2], ahead[c, 2])]
            + [(local[c, 2], ahead_in[j, c, 2]) for j in range(NDIL)])
        for x, (left, right) in enumerate(pairs):
            product = left.astype(f32) * right.astype(f32)
            high = product.astype(bf16)
            low = (product - high.astype(f32)).astype(bf16)
            prods[2 * x * rows:(2 * x + 1) * rows] = high
            prods[(2 * x + 1) * rows:(2 * x + 2) * rows] = low
        sums = dot_nn(prods[...], gather[...])

        def reduced(x):
            return (sums[2 * x * rows:(2 * x + 1) * rows]
                    + sums[(2 * x + 1) * rows:(2 * x + 2) * rows])

        for j in range(NDIL):
            value = reduced(count + 1 + j)
            high = value.astype(bf16).astype(f32)
            dot_out[c, j] = pack(jnp.where(group % 2 == 0, high, value - high))

            @pl.when(i + 2**j < n)
            def _():
                dot_copy(j, c).start()
        for x in range(count + 1):
            kept[c, x] = reduced(x)

        values = softmax_back(
            [reduced(2 * count + j) * scale for j in range(count)],
            [reduced(3 * count + j) for j in range(count)])
        query_part, stack, key_factor = query_grad(values, 1, c)
        value_factor = dot_nn(stack, spread[1])
        q_rows, g_rows = local[c, 1].astype(f32), local[c, 2].astype(f32)
        key_parts = jnp.concatenate(
            [(key_factor[j * rows:(j + 1) * rows] * q_rows).astype(bf16)
             for j in range(count)], axis=0)
        value_parts = jnp.concatenate(
            [(value_factor[j * rows:(j + 1) * rows] * g_rows).astype(bf16)
             for j in range(count)], axis=0)
        projected = dot_nt(key_parts, weights[1]) + dot_nt(value_parts, weights[2])

        def at(slot):
            return projected[(slot + 1) * rows:(slot + 2) * rows]

        for slot in (0, 3):
            part_out[slot, c] = at(slot).astype(bf16)
            give_back(slot, c)
        kept_near[c] = at(1)
        kept_mid[c] = at(2)
        base[c] = projected[:rows] + dot_nt(query_part, weights[0])

    def soften(c):
        for j in range(NDIL):
            @pl.when(i >= 2**j)
            def _():
                dot_copy(j, c).wait_recv()
        packed = dot_in[c].reshape(NDIL * half, LANES)
        folded = [dot_nn(packed, fold[x]) for x in range(2)]
        grad_prob = [kept[c, count]] + [
            jnp.concatenate([f[j * half:(j + 1) * half] for f in folded], axis=0)
            for j in range(NDIL)]
        values = softmax_back([kept[c, j] * scale for j in range(count)], grad_prob)
        for j in range(count):
            prob_out[c, j] = pack(values[j])
        for j in range(NDIL):
            @pl.when(i >= 2**j)
            def _():
                prob_copy(j, c).start()
        add_back(5, c, kept_near)
        part_out[1, c] = kept_near[c].astype(bf16)
        give_back(1, c)

    def finish(c):
        add_back(3, c, kept_mid)
        add_back(4, c, kept_mid)
        part_out[2, c] = kept_mid[c].astype(bf16)
        give_back(2, c)

        packed = prob_out[c].reshape(count * half, LANES)
        halves = []
        for h in range(2):
            at = slice(h * half, (h + 1) * half)
            score = dot_nn(packed, spread[2 * h])
            total = score[:half] * ahead[c, 0, at].astype(f32)
            for j in range(NDIL):
                total += (score[(j + 1) * half:(j + 2) * half]
                          * ahead_in[j, c, 0, at].astype(f32))
            halves.append(total.astype(bf16))
        result = dot_nt(jnp.concatenate(halves, axis=0), weights[0])
        for j in range(NDIL):
            @pl.when(i + 2**j < n)
            def _():
                prob_copy(j, c).wait_recv()
        packed = jnp.concatenate(
            [prob_out[c, 0], prob_in[c].reshape(NDIL * half, LANES)], axis=0)
        for part in range(2):
            halves = []
            for h in range(2):
                at = slice(h * half, (h + 1) * half)
                factor = dot_nn(packed, spread[2 * h + part])
                total = factor[:half] * back[c, part, at].astype(f32)
                for j in range(NDIL):
                    total += (factor[(j + 1) * half:(j + 2) * half]
                              * back_in[j, c, part, at].astype(f32))
                halves.append(total.astype(bf16))
            result += dot_nt(jnp.concatenate(halves, axis=0), weights[1 + part])
        out_ref[0, pl.ds(pl.multiple_of(2 * c * rows, rows), rows), :] = result.astype(bf16)

    def collect(c):
        for kind in (2, 1, 0):
            add_back(kind, c, base)
        out_ref[0, pl.ds(pl.multiple_of((2 * c + 1) * rows, rows), rows), :] = (
            base[c].astype(bf16))

    def step(s, carry):
        def stage(lag, run):
            @pl.when(jnp.logical_and(s >= lag, s < chunks + lag))
            def _():
                run(s - lag)

        stage(LAGS[0], relay_far)
        stage(LAGS[1], relay_near)

        @pl.when(s + AHEAD < chunks)
        def _():
            direct(s + AHEAD)

        stage(LAGS[2], attend)
        stage(LAGS[3], soften)
        stage(LAGS[4], finish)
        stage(LAGS[5], collect)
        return carry

    lax.fori_loop(0, chunks + LAGS[5], step, 0)

    def drain(c, carry):
        for stream in range(2):
            for kind in range(6):
                copy, cond = hop(stream, kind, c)

                @pl.when(cond)
                def _():
                    copy.wait_send()
        for j in range(NDIL):
            for kind, off, cond in returns(j):
                @pl.when(cond)
                def _():
                    back_copy(j, kind, off, c).wait_send()

            @pl.when(i >= 2**j)
            def _():
                prob_copy(j, c).wait_send()

            @pl.when(i + 2**j < n)
            def _():
                dot_copy(j, c).wait_send()
        return carry

    lax.fori_loop(0, chunks, drain, 0)


def per_device(queries, keys, values, grad_out, links, w_query, w_key, w_value):
    frames, patches, width = queries.shape
    n = lax.axis_size("frame")
    rows = 32
    chunks = patches // (2 * rows)
    half = rows // 2
    hbm = pl.BlockSpec(memory_space=pl.ANY)
    f32, bf16 = jnp.float32, jnp.bfloat16
    dma = pltpu.SemaphoreType.DMA
    return pl.pallas_call(
        functools.partial(kernel, n, chunks, rows),
        out_shape=jax.ShapeDtypeStruct((frames, patches, width), bf16),
        in_specs=[pl.BlockSpec(memory_space=pltpu.SMEM)] + [hbm] * 7,
        out_specs=pl.BlockSpec(memory_space=pltpu.VMEM),
        scratch_shapes=[
            pltpu.VMEM((chunks, 3, rows, width), bf16),
            pltpu.VMEM((chunks, 2, rows, width), bf16),
            pltpu.VMEM((chunks, 3, rows, width), bf16),
            pltpu.VMEM((NDIL, chunks, 3, rows, width), bf16),
            pltpu.VMEM((NDIL, chunks, 2, rows, width), bf16),
            pltpu.VMEM((NDIL, chunks, rows, width), bf16),
            pltpu.VMEM((6, chunks, rows, width), bf16),
            pltpu.VMEM((chunks, NDIL + 1, half, LANES), bf16),
            pltpu.VMEM((chunks, NDIL, half, LANES), bf16),
            pltpu.VMEM((chunks, NDIL, half, LANES), bf16),
            pltpu.VMEM((chunks, NDIL, half, LANES), bf16),
            pltpu.VMEM((chunks, NDIL + 2, rows, LANES), f32),
            pltpu.VMEM((chunks, rows, width), f32),
            pltpu.VMEM((chunks, rows, width), f32),
            pltpu.VMEM((chunks, rows, width), f32),
            pltpu.VMEM((8 * (NDIL + 1) * rows, width), bf16),
            pltpu.VMEM((width, LANES), bf16),
            pltpu.VMEM((4, LANES, width), bf16),
            pltpu.VMEM((2, LANES, LANES), bf16),
            pltpu.VMEM((3, width, width), bf16),
            dma((8, chunks)),
            dma((3,)),
            dma((2, 6, chunks)),
            dma((2, NDIL, chunks)),
            dma((NDIL, chunks)),
            dma((NDIL, chunks)),
            dma((NDIL, chunks)),
            dma((NDIL, chunks)),
            dma((NDIL, chunks)),
            dma((6, chunks)),
        ],
        compiler_params=pltpu.CompilerParams(
            collective_id=0, has_side_effects=True, vmem_limit_bytes=60 * 1024 * 1024),
    )(links, queries, keys, values, grad_out, w_query, w_key, w_value)


def solution(mesh):
    placed = (
        P(("dom", "frame"), None, None),
        P(("dom", "frame"), None, None),
        P(("dom", "frame"), None, None),
        P(("dom", "frame"), None, None),
        P(("dom", "frame"), None),
        P(),
        P(),
        P(),
    )
    return jax.shard_map(
        per_device,
        mesh=mesh,
        in_specs=placed,
        out_specs=P(("dom", "frame"), None, None),
        check_vma=False,
    )
```

```python
import functools

import jax
import jax.numpy as jnp
from jax import lax
from jax.experimental import pallas as pl
from jax.experimental.pallas import tpu as pltpu
from jax.sharding import PartitionSpec as P

HEADS = 16
NDIL = 4
LANES = 128
AHEAD = 3
LAGS = (0, 1, 2, 4, 6, 8)


def dot_nn(left, right):
    return lax.dot_general(
        left, right, (((1,), (0,)), ((), ())), preferred_element_type=jnp.float32
    )


def kernel(n, chunks, rows, links_ref, q_ref, k_ref, v_ref, g_ref, wq_ref, wk_ref, wv_ref,
           out_ref, ahead, back, local, ahead_in, back_in, part_out, part_in,
           prob_out, prob_in, dot_out, dot_in, kept, kept_mid, kept_near, base, own_part,
           prods, gather, spread, fold, stored, weights,
           own_sem, w_sem, send_sem, recv_sem, prob_send, prob_recv, dot_send, dot_recv,
           part_send, part_recv):
    width = q_ref.shape[-1]
    head = width // HEADS
    scale = head ** (-0.5)
    half = rows // 2
    count = NDIL + 1
    i = lax.axis_index("frame")
    f32, bf16 = jnp.float32, jnp.bfloat16

    own = (ahead, back)
    slots = (ahead_in, back_in)

    def place(stream):
        return (i, 1) if stream == 0 else (n - 1 - i, -1)

    def loads(c):
        plan = ((k_ref, 0, ahead, 0), (k_ref, 1, ahead, 1), (v_ref, 1, ahead, 2),
                (q_ref, 0, back, 0), (g_ref, 0, back, 1),
                (v_ref, 0, local, 0), (q_ref, 1, local, 1), (g_ref, 1, local, 2))
        return [pltpu.make_async_copy(
            src.at[0, pl.ds(pl.multiple_of((2 * c + side) * rows, rows), rows), :],
            dst.at[c, part], own_sem.at[x, c])
            for x, (src, side, dst, part) in enumerate(plan)]

    def hop(stream, kind, c):
        m, sign = place(stream)
        bit1, bit0 = (m // 2) % 2, m % 2
        mine, into = own[stream].at[c], slots[stream]
        src, slot, off, cond = (
            (mine, 2, 4, m + 4 < n),
            (mine, 1, 2, bit1 == 0),
            (mine, 0, 1, bit0 == 0),
            (into.at[2, c], 3, 4, jnp.logical_and(m >= 4, m + 4 < n)),
            (into.at[2, c], 1, -2, jnp.logical_and(m >= 4, bit1 == 1)),
            (into.at[1, c], 0, -1, jnp.logical_and(m >= 2, bit0 == 1)),
        )[kind]
        copy = pltpu.make_async_remote_copy(
            src_ref=src, dst_ref=into.at[slot, c],
            send_sem=send_sem.at[stream, kind, c], recv_sem=recv_sem.at[stream, slot, c],
            device_id={"frame": i + sign * off}, device_id_type=pl.DeviceIdType.MESH)
        return copy, cond

    def send(stream, kind, c):
        copy, cond = hop(stream, kind, c)

        @pl.when(cond)
        def _():
            copy.start()

    def arrive(stream, slot, c):
        m, sign = place(stream)

        @pl.when(m >= 2**slot)
        def _():
            pltpu.make_async_remote_copy(
                src_ref=own[stream].at[c], dst_ref=slots[stream].at[slot, c],
                send_sem=send_sem.at[stream, 0, c], recv_sem=recv_sem.at[stream, slot, c],
                device_id={"frame": i - sign * 2**slot},
                device_id_type=pl.DeviceIdType.MESH).wait_recv()

    def returns(slot):
        bit1, bit0 = (i // 2) % 2, i % 2
        if slot == 2:
            return [(0, -4, i >= 4)]
        if slot == 3:
            return [(3, -4, i >= 8)]
        if slot == 1:
            return [(1, -2, jnp.logical_and(i >= 2, bit1 == 1)),
                    (4, 2, jnp.logical_and(i >= 2, bit1 == 0))]
        return [(2, -1, bit0 == 1), (5, 1, jnp.logical_and(i >= 1, bit0 == 0))]

    def back_copy(slot, kind, off, c):
        return pltpu.make_async_remote_copy(
            src_ref=part_out.at[slot, c], dst_ref=part_in.at[kind, c],
            send_sem=part_send.at[slot, c], recv_sem=part_recv.at[kind, c],
            device_id={"frame": i + off}, device_id_type=pl.DeviceIdType.MESH)

    def give_back(slot, c):
        for kind, off, cond in returns(slot):
            @pl.when(cond)
            def _():
                back_copy(slot, kind, off, c).start()

    def add_back(kind, c, ref):
        cond = hop(0, kind, c)[1]
        off = (4, 2, 1, 4, -2, -1)[kind]

        @pl.when(cond)
        def _():
            pltpu.make_async_remote_copy(
                src_ref=part_out.at[0, c], dst_ref=part_in.at[kind, c],
                send_sem=part_send.at[0, c], recv_sem=part_recv.at[kind, c],
                device_id={"frame": i + off},
                device_id_type=pl.DeviceIdType.MESH).wait_recv()
            ref[c] += part_in[kind, c].astype(f32)

    def prob_copy(j, c):
        return pltpu.make_async_remote_copy(
            src_ref=prob_out.at[c, j + 1], dst_ref=prob_in.at[c, j],
            send_sem=prob_send.at[j, c], recv_sem=prob_recv.at[j, c],
            device_id={"frame": i - 2**j}, device_id_type=pl.DeviceIdType.MESH)

    def dot_copy(j, c):
        return pltpu.make_async_remote_copy(
            src_ref=dot_out.at[c, j], dst_ref=dot_in.at[c, j],
            send_sem=dot_send.at[j, c], recv_sem=dot_recv.at[j, c],
            device_id={"frame": i + 2**j}, device_id_type=pl.DeviceIdType.MESH)

    for c in range(chunks):
        for copy in loads(c):
            copy.start()
    w_copies = [pltpu.make_async_copy(w, stored.at[x], w_sem.at[x])
                for x, w in enumerate((wq_ref, wk_ref, wv_ref))]
    for copy in w_copies:
        copy.start()

    barrier = pltpu.get_barrier_semaphore()
    peers = jnp.int32(0)
    for j in range(NDIL):
        for off in (2**j, -(2**j)):
            there = jnp.logical_and(i + off >= 0, i + off < n)
            peers = peers + there.astype(jnp.int32)

            @pl.when(there)
            def _():
                pl.semaphore_signal(barrier, inc=1, device_id={"frame": i + off},
                                    device_id_type=pl.DeviceIdType.MESH)
    pl.semaphore_wait(barrier, peers)

    def direct(c):
        for copy in loads(c):
            copy.wait()
        for kind in range(3):
            for stream in range(2):
                send(stream, kind, c)

    for c in range(min(AHEAD, chunks)):
        direct(c)

    feature = lax.broadcasted_iota(jnp.int32, (width, LANES), 0) // head
    lane = lax.broadcasted_iota(jnp.int32, (width, LANES), 1) % HEADS
    gather[...] = jnp.where(feature == lane, 1.0, 0.0).astype(bf16)
    lane = lax.broadcasted_iota(jnp.int32, (LANES, width), 0)
    feature = lax.broadcasted_iota(jnp.int32, (LANES, width), 1) // head
    for x in range(4):
        hit = jnp.logical_and(lane % HEADS == feature, lane // (2 * HEADS) == x)
        spread[x] = jnp.where(hit, 1.0, 0.0).astype(bf16)
    lane = lax.broadcasted_iota(jnp.int32, (LANES, LANES), 0)
    feature = lax.broadcasted_iota(jnp.int32, (LANES, LANES), 1)
    for x in range(2):
        hit = jnp.logical_and(lane % HEADS == feature % HEADS, lane // (2 * HEADS) == 2 * x)
        fold[x] = jnp.where(hit, 1.0, 0.0).astype(bf16)

    for j in range(NDIL):
        @pl.when(i < 2**j)
        def _():
            for c in range(chunks):
                for part in range(3):
                    ahead_in[j, c, part] = jnp.zeros((rows, width), bf16)
                dot_in[c, j] = jnp.zeros((half, LANES), bf16)

        @pl.when(i + 2**j >= n)
        def _():
            for c in range(chunks):
                for part in range(2):
                    back_in[j, c, part] = jnp.zeros((rows, width), bf16)
                prob_in[c, j] = jnp.zeros((half, LANES), bf16)
    lanes = lax.broadcasted_iota(jnp.int32, (rows, LANES), 1)
    group = (lanes // HEADS) % 4
    lower = lanes[:half] < LANES // 2

    def pack(value):
        return jnp.where(lower, value[:half], value[half:]).astype(bf16)

    def softmax_back(scores, grad_prob):
        live = [None] + [(links_ref[0, j] > 0).astype(f32) for j in range(NDIL)]
        scores = [s if j == 0 else jnp.where(live[j] > 0, s, -1e30)
                  for j, s in enumerate(scores)]
        highest = functools.reduce(jnp.maximum, scores)
        raw = [jnp.exp(s - highest) for s in scores]
        raw = [r if j == 0 else r * live[j] for j, r in enumerate(raw)]
        total = functools.reduce(jnp.add, raw)
        probability = [r / total for r in raw]
        inner = functools.reduce(
            jnp.add, [p * g for p, g in zip(probability, grad_prob)])
        values = []
        for prob, grad in zip(probability, grad_prob):
            grad_score = prob * (grad - inner) * scale
            value = jnp.where(group < 2, grad_score, prob)
            high = value.astype(bf16).astype(f32)
            values.append(jnp.where(group % 2 == 0, high, value - high))
        return values

    def relay_far(c):
        for stream in range(2):
            arrive(stream, 2, c)
            send(stream, 4, c)
            send(stream, 3, c)

    def relay_near(c):
        for stream in range(2):
            arrive(stream, 1, c)
            send(stream, 5, c)

    def query_grad(values, part, c):
        stack = jnp.concatenate([v.astype(bf16) for v in values], axis=0)
        factor = dot_nn(stack, spread[0])
        total = factor[:rows] * ahead[c, part].astype(f32)
        for j in range(NDIL):
            total += (factor[(j + 1) * rows:(j + 2) * rows]
                      * ahead_in[j, c, part].astype(f32))
        return total.astype(bf16), stack, factor

    def attend(c):
        for slot in (0, 3):
            for stream in range(2):
                arrive(stream, slot, c)
        pairs = (
            [(back[c, 0], ahead[c, 0])]
            + [(back[c, 0], ahead_in[j, c, 0]) for j in range(NDIL)]
            + [(back[c, 1], local[c, 0])]
            + [(back_in[j, c, 1], local[c, 0]) for j in range(NDIL)]
            + [(local[c, 1], ahead[c, 1])]
            + [(local[c, 1], ahead_in[j, c, 1]) for j in range(NDIL)]
            + [(local[c, 2], ahead[c, 2])]
            + [(local[c, 2], ahead_in[j, c, 2]) for j in range(NDIL)])
        for x, (left, right) in enumerate(pairs):
            product = left.astype(f32) * right.astype(f32)
            high = product.astype(bf16)
            low = (product - high.astype(f32)).astype(bf16)
            prods[2 * x * rows:(2 * x + 1) * rows] = high
            prods[(2 * x + 1) * rows:(2 * x + 2) * rows] = low
        sums = dot_nn(prods[...], gather[...])

        def reduced(x):
            return (sums[2 * x * rows:(2 * x + 1) * rows]
                    + sums[(2 * x + 1) * rows:(2 * x + 2) * rows])

        for j in range(NDIL):
            value = reduced(count + 1 + j)
            high = value.astype(bf16).astype(f32)
            dot_out[c, j] = pack(jnp.where(group % 2 == 0, high, value - high))

            @pl.when(i + 2**j < n)
            def _():
                dot_copy(j, c).start()
        for x in range(count + 1):
            kept[c, x] = reduced(x)

        values = softmax_back(
            [reduced(2 * count + j) * scale for j in range(count)],
            [reduced(3 * count + j) for j in range(count)])
        query_part, stack, key_factor = query_grad(values, 1, c)
        value_factor = dot_nn(stack, spread[1])
        q_rows, g_rows = local[c, 1].astype(f32), local[c, 2].astype(f32)
        key_parts = jnp.concatenate(
            [(key_factor[j * rows:(j + 1) * rows] * q_rows).astype(bf16)
             for j in range(count)], axis=0)
        value_parts = jnp.concatenate(
            [(value_factor[j * rows:(j + 1) * rows] * g_rows).astype(bf16)
             for j in range(count)], axis=0)
        projected = (dot_nn(key_parts[rows:], weights[1])
                     + dot_nn(value_parts[rows:], weights[2]))

        def at(slot):
            return projected[slot * rows:(slot + 1) * rows]

        for slot in (0, 3):
            part_out[slot, c] = at(slot).astype(bf16)
            give_back(slot, c)
        kept_near[c] = at(1)
        kept_mid[c] = at(2)
        own_part[c, 0] = query_part
        own_part[c, 1] = key_parts[:rows]
        own_part[c, 2] = value_parts[:rows]

    def soften(c):
        for j in range(NDIL):
            @pl.when(i >= 2**j)
            def _():
                dot_copy(j, c).wait_recv()
        packed = dot_in[c].reshape(NDIL * half, LANES)
        folded = [dot_nn(packed, fold[x]) for x in range(2)]
        grad_prob = [kept[c, count]] + [
            jnp.concatenate([f[j * half:(j + 1) * half] for f in folded], axis=0)
            for j in range(NDIL)]
        values = softmax_back([kept[c, j] * scale for j in range(count)], grad_prob)
        for j in range(count):
            prob_out[c, j] = pack(values[j])
        for j in range(NDIL):
            @pl.when(i >= 2**j)
            def _():
                prob_copy(j, c).start()
        add_back(5, c, kept_near)
        part_out[1, c] = kept_near[c].astype(bf16)
        give_back(1, c)

    def finish(c):
        add_back(3, c, kept_mid)
        add_back(4, c, kept_mid)
        part_out[2, c] = kept_mid[c].astype(bf16)
        give_back(2, c)

        packed = prob_out[c].reshape(count * half, LANES)
        halves = []
        for h in range(2):
            at = slice(h * half, (h + 1) * half)
            score = dot_nn(packed, spread[2 * h])
            total = score[:half] * ahead[c, 0, at].astype(f32)
            for j in range(NDIL):
                total += (score[(j + 1) * half:(j + 2) * half]
                          * ahead_in[j, c, 0, at].astype(f32))
            halves.append(total.astype(bf16))
        result = dot_nn(jnp.concatenate(halves + [own_part[c, 0]], axis=0), weights[0])
        for j in range(NDIL):
            @pl.when(i + 2**j < n)
            def _():
                prob_copy(j, c).wait_recv()
        packed = jnp.concatenate(
            [prob_out[c, 0], prob_in[c].reshape(NDIL * half, LANES)], axis=0)
        for part in range(2):
            halves = []
            for h in range(2):
                at = slice(h * half, (h + 1) * half)
                factor = dot_nn(packed, spread[2 * h + part])
                total = factor[:half] * back[c, part, at].astype(f32)
                for j in range(NDIL):
                    total += (factor[(j + 1) * half:(j + 2) * half]
                              * back_in[j, c, part, at].astype(f32))
                halves.append(total.astype(bf16))
            result += dot_nn(
                jnp.concatenate(halves + [own_part[c, 1 + part]], axis=0), weights[1 + part])
        out_ref[0, pl.ds(pl.multiple_of(2 * c * rows, rows), rows), :] = (
            result[:rows].astype(bf16))
        base[c] = result[rows:]

    def collect(c):
        for kind in (2, 1, 0):
            add_back(kind, c, base)
        out_ref[0, pl.ds(pl.multiple_of((2 * c + 1) * rows, rows), rows), :] = (
            base[c].astype(bf16))

    def step(s, carry):
        def stage(lag, run):
            @pl.when(jnp.logical_and(s >= lag, s < chunks + lag))
            def _():
                run(s - lag)

        stage(LAGS[0], relay_far)
        stage(LAGS[1], relay_near)

        @pl.when(s + AHEAD < chunks)
        def _():
            direct(s + AHEAD)

        for x, when in ((1, 0), (2, 1), (0, 2)):
            @pl.when(s == when)
            def _():
                w_copies[x].wait()
                weights[x] = stored[x].T

        stage(LAGS[2], attend)
        stage(LAGS[3], soften)
        stage(LAGS[4], finish)
        stage(LAGS[5], collect)
        return carry

    lax.fori_loop(0, chunks + LAGS[5], step, 0)

    def drain(c, carry):
        for stream in range(2):
            for kind in range(6):
                copy, cond = hop(stream, kind, c)

                @pl.when(cond)
                def _():
                    copy.wait_send()
        for j in range(NDIL):
            for kind, off, cond in returns(j):
                @pl.when(cond)
                def _():
                    back_copy(j, kind, off, c).wait_send()

            @pl.when(i >= 2**j)
            def _():
                prob_copy(j, c).wait_send()

            @pl.when(i + 2**j < n)
            def _():
                dot_copy(j, c).wait_send()
        return carry

    lax.fori_loop(0, chunks, drain, 0)


def per_device(queries, keys, values, grad_out, links, w_query, w_key, w_value):
    frames, patches, width = queries.shape
    n = lax.axis_size("frame")
    rows = 32
    chunks = patches // (2 * rows)
    half = rows // 2
    hbm = pl.BlockSpec(memory_space=pl.ANY)
    f32, bf16 = jnp.float32, jnp.bfloat16
    dma = pltpu.SemaphoreType.DMA
    return pl.pallas_call(
        functools.partial(kernel, n, chunks, rows),
        out_shape=jax.ShapeDtypeStruct((frames, patches, width), bf16),
        in_specs=[pl.BlockSpec(memory_space=pltpu.SMEM)] + [hbm] * 7,
        out_specs=pl.BlockSpec(memory_space=pltpu.VMEM),
        scratch_shapes=[
            pltpu.VMEM((chunks, 3, rows, width), bf16),
            pltpu.VMEM((chunks, 2, rows, width), bf16),
            pltpu.VMEM((chunks, 3, rows, width), bf16),
            pltpu.VMEM((NDIL, chunks, 3, rows, width), bf16),
            pltpu.VMEM((NDIL, chunks, 2, rows, width), bf16),
            pltpu.VMEM((NDIL, chunks, rows, width), bf16),
            pltpu.VMEM((6, chunks, rows, width), bf16),
            pltpu.VMEM((chunks, NDIL + 1, half, LANES), bf16),
            pltpu.VMEM((chunks, NDIL, half, LANES), bf16),
            pltpu.VMEM((chunks, NDIL, half, LANES), bf16),
            pltpu.VMEM((chunks, NDIL, half, LANES), bf16),
            pltpu.VMEM((chunks, NDIL + 2, rows, LANES), f32),
            pltpu.VMEM((chunks, rows, width), f32),
            pltpu.VMEM((chunks, rows, width), f32),
            pltpu.VMEM((chunks, rows, width), f32),
            pltpu.VMEM((chunks, 3, rows, width), bf16),
            pltpu.VMEM((8 * (NDIL + 1) * rows, width), bf16),
            pltpu.VMEM((width, LANES), bf16),
            pltpu.VMEM((4, LANES, width), bf16),
            pltpu.VMEM((2, LANES, LANES), bf16),
            pltpu.VMEM((3, width, width), bf16),
            pltpu.VMEM((3, width, width), bf16),
            dma((8, chunks)),
            dma((3,)),
            dma((2, 6, chunks)),
            dma((2, NDIL, chunks)),
            dma((NDIL, chunks)),
            dma((NDIL, chunks)),
            dma((NDIL, chunks)),
            dma((NDIL, chunks)),
            dma((NDIL, chunks)),
            dma((6, chunks)),
        ],
        compiler_params=pltpu.CompilerParams(
            collective_id=0, has_side_effects=True, vmem_limit_bytes=60 * 1024 * 1024),
    )(links, queries, keys, values, grad_out, w_query, w_key, w_value)


def solution(mesh):
    placed = (
        P(("dom", "frame"), None, None),
        P(("dom", "frame"), None, None),
        P(("dom", "frame"), None, None),
        P(("dom", "frame"), None, None),
        P(("dom", "frame"), None),
        P(),
        P(),
        P(),
    )
    return jax.shard_map(
        per_device,
        mesh=mesh,
        in_specs=placed,
        out_specs=P(("dom", "frame"), None, None),
        check_vma=False,
    )
```
